32 devices in a mesh: group: 2 (over x), expert: 16 (over z, y, core), tensor: 1.
Axes of the slice: x: 2, y: 2, z: 4, core: 2. Of those that a mesh axis runs over, the one named last changes fastest.
Arguments:
- tokens: bfloat16 [1024, 4096], P(('group', 'expert', 'tensor')), parts along dimension 0, may hold values from -600 to 600
- norm_gain: float32 [4096], replicated, may hold values from 0.1 to 1.9
- w_gate: bfloat16 [16, 4096, 768], P('expert', None, 'tensor'), may hold values from -0.09375 to 0.09375
- w_up: bfloat16 [16, 4096, 768], P('expert', None, 'tensor'), may hold values from -0.09375 to 0.09375
- w_down: bfloat16 [16, 768, 4096], P('expert', 'tensor'), may hold values from -0.4375 to 0.4375
- expert_ids: int32 [1024, 8], P(('group', 'expert', 'tensor')), parts along dimension 0, may hold values from 0 to 15, all different within a row; in each aligned block of 32 rows (0 to 31, 32 to 63, ...) at most 32 rows name the same one
- route_weights: float32 [1024, 8], P(('group', 'expert', 'tensor')), parts along dimension 0, may hold values from 0.05 to 1
Outputs:
- mixed: bfloat16 [1024, 4096], P(('group', 'expert', 'tensor')), parts along dimension 0
The draws below stay inside these ranges and needn't reach their ends.
There are 2 independent parts, one for each index of `group`. The reference program is written for one: setup_inputs(seed, part) draws one part's arguments, and reference() takes and returns one part's arrays. A program takes and returns all parts, laid end to end along the dimension named above; an argument that names none is the same for every part. Nothing has to cross between parts.
Inputs may be any that keep to these rules, and one draw needn't show every extreme that they name: `expert_ids`: each row names 8 different experts. Among the 32 rows of one device no expert is named more than 32 times, and in every draw some device names some expert exactly 32 times.
All inputs are finite; a program needn't handle non-finite values.
Results may differ from the reference program's by a relative error of at most 0.0077.
Values may be sent and summed in bfloat16 or wider, within the bound.
A program may use at most 128 MiB of HBM per device.

```python
import math
import jax
import jax.numpy as jnp
import numpy as np
from jax import lax

D = 4096
EXPERT_FF = 768
TOPK = 8
TOK_DEV = 32
EXPERTS = 16
CAP = 32
TOKENS = 512
N_EXPERT = 16
N_TENSOR = 1


def draw_tokens(key, part):
    first, second, third = jax.random.split(jax.random.fold_in(key, 7), 3)
    base = jnp.clip(jax.random.normal(first, (TOKENS, D), jnp.float32), -6.0, 6.0)
    columns = jnp.exp(jax.random.uniform(second, (1, D), jnp.float32, 0.0, math.log(10.0)))
    rowscale = jnp.exp(jax.random.uniform(third, (TOKENS, 1), jnp.float32, 0.0, math.log(10.0)))
    return (base * columns * rowscale).astype(jnp.bfloat16)


def level_of(stream_key, dims, shards, least, largest):
    def one(dim, shards_of):
        draws = jax.random.uniform(jax.random.fold_in(jax.random.fold_in(stream_key, 6), dim), (shards_of,), jnp.float32, least / len(shards), largest / len(shards))
        return jnp.repeat(jnp.exp(draws), dims[dim] // shards_of).reshape((-1,) + (1,) * (len(dims) - dim - 1))

    loudness = one(*shards[0])
    for cut in shards[1:]:
        loudness = loudness * one(*cut)
    return loudness


def deal_out(key, own, number, rows, count, top, reach, skew):
    ranking = jax.random.permutation(key, count)
    crowded, usual = portions_of(count, rows * top, reach, skew, True), portions_of(count, rows * top, reach, skew, False)
    places = jnp.arange(count)

    def named(tallies, offset_by):
        used = int((tallies > 0).sum())
        fixed = max(1, used // 4)
        passed = fixed + (places - fixed + offset_by * (used - fixed)) % max(1, count - fixed)
        return jnp.zeros((count,), jnp.int32).at[ranking[jnp.where(places < fixed, places, passed)]].set(jnp.asarray(tallies, jnp.int32))

    tallies = jnp.where(number % 4 == 0, named(crowded, number // 4), named(usual, number - number // 4 - 1))
    mixed = jax.random.permutation(jax.random.fold_in(own, 3), count)
    donor, taker = mixed[0:count // 2 * 2:2], mixed[1:count // 2 * 2:2]
    margin = jnp.minimum(tallies[donor] - 1, reach - tallies[taker]) // 2
    margin = jnp.where((donor == ranking[0]) | (taker == ranking[0]) | (tallies[taker] == 0), 0, jnp.maximum(margin, 0))
    passed = jax.random.randint(jax.random.fold_in(own, 4), (count // 2,), 0, 1 << 20) % (margin + 1)
    tallies = tallies.at[donor].add(-passed).at[taker].add(passed)
    labels = jnp.searchsorted(jnp.cumsum(tallies), jnp.arange(rows * top), side="right").astype(jnp.int32)
    table = labels.reshape(top, rows).T
    table = table[jax.random.permutation(jax.random.fold_in(own, 1), rows)]
    offset_by = jax.random.randint(jax.random.fold_in(own, 2), (rows, 1), 0, top)
    return jnp.take_along_axis(table, (jnp.arange(top)[None, :] + offset_by) % top, axis=1)


def portions_of(amount, total, bound, lean, full):
    portions = [(1 << 20) // math.isqrt(rank ** lean) + 1 for rank in range(1, amount + 1)]
    largest = bound if full else min(bound, max(-(-total // amount), total * portions[0] // sum(portions)))
    least = 1 if total - largest >= amount - 1 else 0
    holding, surplus = [largest] + [least] * (amount - 1), total - largest - least * (amount - 1)
    while surplus > 0:
        free = [i for i in range(1, amount) if holding[i] < largest] or [i for i in range(1, amount) if holding[i] < bound]
        mass, left = sum([portions[i] for i in free]), surplus
        for i in free:
            extra = min(bound - holding[i], max(1, left * portions[i] // mass), surplus)
            holding[i] = holding[i] + extra
            surplus = surplus - extra
    return np.array(holding)


def centred(key, shape, deviation, most, cuts=(), kind=jnp.bfloat16):
    loudness = level_of(key, shape, cuts, -0.22, 0.18) if cuts else 1.0
    result = jax.random.normal(key, shape, jnp.float32) * deviation * loudness
    return jnp.minimum(jnp.maximum(result, -most), most).astype(kind)


def setup_inputs(seed: int = 0, part: int = 0) -> dict:
    key_list = jax.random.split(jax.random.key(seed), 8)
    part_splits = jax.random.split(jax.random.fold_in(key_list[7], part), 8)
    tokens = draw_tokens(jax.random.fold_in(jax.random.fold_in(key_list[7], part), 71), part)
    norm_gain = jnp.clip(1.0 + 0.18 * jax.random.normal(key_list[1], (D,), jnp.float32), 0.1, 1.9)
    w_gate = centred(key_list[2], (EXPERTS, D, EXPERT_FF), D ** -0.5, 0.09375, ((0, 16),))
    w_up = centred(key_list[3], (EXPERTS, D, EXPERT_FF), D ** -0.5, 0.09375, ((0, 16),))
    w_down = centred(key_list[4], (EXPERTS, EXPERT_FF, D), (EXPERT_FF // 4) ** -0.5, 0.4375, ((0, 16),))
    expert_ids_keys = jax.random.split(jax.random.fold_in(part_splits[5], 1), TOKENS // TOK_DEV)
    expert_ids_turns = jax.random.permutation(jax.random.fold_in(part_splits[5], 3), TOKENS // TOK_DEV)
    expert_ids = jax.vmap(lambda own, number: deal_out(jax.random.fold_in(part_splits[5], 2), own, number, TOK_DEV, EXPERTS, TOPK, CAP, 2))(expert_ids_keys, expert_ids_turns).reshape((TOKENS, TOPK))
    route_weights = jnp.clip(jnp.exp(math.log(1.0) - 2.9957323 * jax.random.uniform(part_splits[6], (TOKENS, TOPK), jnp.float32) ** level_of(part_splits[6], (TOKENS, TOPK), ((0, 16),), -0.2, 0.2)), 0.05, 1.0)
    return {"tokens": tokens, "norm_gain": norm_gain, "w_gate": w_gate, "w_up": w_up, "w_down": w_down, "expert_ids": expert_ids, "route_weights": route_weights}


epsilon = 1e-06

def reference(tokens, norm_gain, w_gate, w_up, w_down, expert_ids, route_weights):
    stream = tokens.astype(jnp.float32)
    normed = (stream * lax.rsqrt(lax.optimization_barrier(jnp.mean(stream * stream, axis=-1, keepdims=True)) + epsilon) * norm_gain).astype(jnp.bfloat16)
    route = route_weights / lax.optimization_barrier(jnp.sum(route_weights, axis=-1, keepdims=True))
    flat_ids = expert_ids.reshape(-1).astype(jnp.int32)
    flat_route = route.reshape(-1)
    row_total = flat_ids.shape[0]
    row_bound = CAP * N_EXPERT * N_TENSOR
    half_units = EXPERT_FF // N_TENSOR
    position = jnp.arange(row_total, dtype=jnp.int32)

    def per_expert(running, expert):
        sort_key = jnp.where(flat_ids == expert, position, position + row_total)
        chosen = jnp.argsort(sort_key)[:row_bound].astype(jnp.int32)
        is_valid = flat_ids[chosen] == expert
        owner_row = (chosen // TOPK).astype(jnp.int32)
        rows_in = normed[owner_row]
        gate_cols = w_gate[expert]
        up_cols = w_up[expert]
        down_rows = w_down[expert]
        expert_sum = jnp.zeros((row_bound, D), jnp.float32)
        for core_index in range(N_TENSOR):
            low = core_index * half_units
            gate_pre = jnp.dot(rows_in, gate_cols[:, low:low + half_units], preferred_element_type=jnp.float32)
            up_pre = jnp.dot(rows_in, up_cols[:, low:low + half_units], preferred_element_type=jnp.float32)
            hidden = (jax.nn.silu(gate_pre) * up_pre).astype(jnp.bfloat16)
            partial_value = jnp.dot(hidden, down_rows[low:low + half_units, :], preferred_element_type=jnp.float32)
            rounded = lax.optimization_barrier(partial_value.astype(jnp.bfloat16))
            expert_sum = expert_sum + rounded.astype(jnp.float32)
        expert_out = lax.optimization_barrier(expert_sum.astype(jnp.bfloat16)).astype(jnp.float32)
        row_weight = jnp.where(is_valid, flat_route[chosen], jnp.float32(0.0))
        running = running.at[owner_row].add(row_weight[:, None] * expert_out)
        return (running, None)
    running, _ = lax.scan(per_expert, jnp.zeros((TOKENS, D), jnp.float32), jnp.arange(EXPERTS, dtype=jnp.int32))
    return running.astype(jnp.bfloat16)
```

```python
import jax
import jax.numpy as jnp
from jax import lax
from jax.sharding import PartitionSpec as P

epsilon = 1e-06
AXES = ("expert", "tensor")


def shards(tokens, norm_gain, w_gate, w_up, w_down, expert_ids, route_weights):
    row_count, feature_count = tokens.shape
    experts = lax.axis_size("expert")
    stream = tokens.astype(jnp.float32)
    normed = (
        stream * lax.rsqrt(jnp.mean(stream * stream, axis=-1, keepdims=True) + epsilon) * norm_gain
    ).astype(jnp.bfloat16)
    route = route_weights / jnp.sum(route_weights, axis=-1, keepdims=True)
    chosen = expert_ids[:, :, None] == jnp.arange(experts, dtype=jnp.int32)[None, None, :]
    table = jnp.sum(jnp.where(chosen, route[:, :, None], 0.0), axis=1)
    tables = lax.all_gather(table, AXES, axis=0, tiled=True)
    rows = lax.all_gather(normed, AXES, axis=0, tiled=True)
    me = lax.axis_index("expert")
    mine = jnp.arange(experts, dtype=jnp.int32)[None, :] == me
    weight = jnp.sum(jnp.where(mine, tables, 0.0), axis=1, keepdims=True)
    gate_pre = jnp.dot(rows, w_gate[0], preferred_element_type=jnp.float32)
    up_pre = jnp.dot(rows, w_up[0], preferred_element_type=jnp.float32)
    hidden = (jax.nn.silu(gate_pre) * up_pre).astype(jnp.bfloat16)
    out = jnp.dot(hidden, w_down[0], preferred_element_type=jnp.float32) * weight
    return lax.psum_scatter(out.astype(jnp.bfloat16), AXES, scatter_dimension=0, tiled=True)


def solution(mesh):
    in_specs = (
        P(("group", "expert", "tensor"), None),
        P(),
        P("expert", None, "tensor"),
        P("expert", None, "tensor"),
        P("expert", "tensor", None),
        P(("group", "expert", "tensor"), None),
        P(("group", "expert", "tensor"), None),
    )
    out_specs = P(("group", "expert", "tensor"), None)
    return jax.shard_map(shards, mesh=mesh, in_specs=in_specs, out_specs=out_specs, check_vma=False)
```

```python
import functools
import jax
import jax.numpy as jnp
from jax import lax
from jax.experimental import pallas as pl
from jax.experimental.pallas import tpu as pltpu
from jax.sharding import PartitionSpec as P

epsilon = 1e-06
AXES = ("expert", "tensor")
MESH = pl.DeviceIdType.MESH
RIGHT, LEFT = 0, 1


class Ring:
    def __init__(self, experts):
        self.pairs = experts // 2
        self.line = self.pairs // 2
        self.group = lax.axis_index("group")
        self.me = lax.axis_index("expert")
        self.core = self.me % 2
        pair = self.me // 2
        row, side = pair // 2, pair % 2
        self.pos = (1 - side) * row + side * (self.pairs - 1 - row)

    def at(self, offset, core=None):
        core = self.core if core is None else core
        place = (self.pos + offset + 2 * self.pairs) % self.pairs
        side = place // self.line
        row = (1 - side) * place + side * (self.pairs - 1 - place)
        return (row * 2 + side) * 2 + core

    def target(self, expert):
        return (self.group, expert, 0)


def meet(ring, partners):
    barrier = pltpu.get_barrier_semaphore()
    for expert in partners:
        pl.semaphore_signal(barrier, inc=1, device_id=ring.target(expert), device_id_type=MESH)
    pl.semaphore_wait(barrier, len(partners))


def remote(ring, src, dst, send_sem, recv_sem, expert):
    return pltpu.make_async_remote_copy(
        src_ref=src,
        dst_ref=dst,
        send_sem=send_sem,
        recv_sem=recv_sem,
        device_id=ring.target(expert),
        device_id_type=MESH,
    )


def runs(direction, half, distance, reach):
    return distance < reach or (distance == reach and half == direction)


def gather_kernel(
    experts, x_ref, t_ref, g_ref, w_ref, ring_send, ring_recv, pair_send, pair_recv, t_send, t_recv, own_sem
):
    ring = Ring(experts)
    reach = ring.pairs // 2
    rows = x_ref.shape[0] // 2
    sibling = ring.at(0, 1 - ring.core)
    peers = [(ring.me + k) % experts for k in range(1, experts)]
    meet(ring, peers)

    def part(ref, h):
        return ref.at[pl.ds(rows * h, rows)]

    def slot(expert, h):
        return g_ref.at[expert, pl.ds(rows * h, rows)]

    sign = (-1, 1)
    sent = []

    def ring_copy(direction, step, h):
        expert = ring.at(sign[direction] * (step - 1))
        src = part(x_ref, h) if step == 1 else slot(expert, h)
        return remote(
            ring,
            src,
            slot(expert, h),
            ring_send.at[direction, step - 1, h],
            ring_recv.at[direction, step - 1, h],
            ring.at(-sign[direction]),
        )

    def ring_arrival(direction, step, h):
        here = slot(ring.at(sign[direction] * step), h)
        return remote(
            ring,
            here,
            here,
            ring_send.at[direction, step - 1, h],
            ring_recv.at[direction, step - 1, h],
            ring.at(-sign[direction]),
        )

    def pair_copy(offset, h):
        expert = ring.at(offset)
        src = part(x_ref, h) if offset == 0 else slot(expert, h)
        index = offset % ring.pairs
        return remote(ring, src, slot(expert, h), pair_send.at[index, h], pair_recv.at[index, h], sibling)

    def pair_arrival(offset, h):
        here = slot(ring.at(offset, 1 - ring.core), h)
        index = offset % ring.pairs
        return remote(ring, here, here, pair_send.at[index, h], pair_recv.at[index, h], sibling)

    def go(copy):
        copy.start()
        sent.append(copy)

    for h in range(2):
        for direction in (RIGHT, LEFT):
            go(ring_copy(direction, 1, h))
    for h in range(2):
        go(pair_copy(0, h))
    for k in range(1, experts):
        to = (ring.me + k) % experts
        go(remote(ring, t_ref.at[to], w_ref.at[ring.me], t_send.at[k - 1], t_recv.at[k - 1], to))
    own = pltpu.make_async_copy(x_ref, g_ref.at[ring.me], own_sem.at[0])
    own.start()
    own_table = pltpu.make_async_copy(t_ref.at[ring.me], w_ref.at[ring.me], own_sem.at[1])
    own_table.start()
    forwarded = [(0, 0), (0, 1)]
    for step in range(1, reach + 1):
        for h in range(2):
            for direction in (RIGHT, LEFT):
                if not runs(direction, h, step, reach):
                    continue
                ring_arrival(direction, step, h).wait_recv()
                if runs(direction, h, step + 1, reach):
                    go(ring_copy(direction, step + 1, h))
                go(pair_copy(sign[direction] * step, h))
                forwarded.append((sign[direction] * step, h))
    for offset, h in forwarded:
        pair_arrival(offset, h).wait_recv()
    for k in range(1, experts):
        origin = (ring.me + experts - k) % experts
        here = w_ref.at[origin]
        remote(ring, here, here, t_send.at[k - 1], t_recv.at[k - 1], origin).wait_recv()
    own.wait()
    own_table.wait()
    for copy in sent:
        copy.wait_send()


def gather_rows(experts, normed, table):
    rows, features = normed.shape
    pairs, reach = experts // 2, experts // 4
    vmem = pl.BlockSpec(memory_space=pltpu.VMEM)
    return pl.pallas_call(
        functools.partial(gather_kernel, experts),
        out_shape=(
            jax.ShapeDtypeStruct((experts, rows, features), normed.dtype),
            jax.ShapeDtypeStruct(table.shape, table.dtype),
        ),
        in_specs=[vmem, vmem],
        out_specs=(vmem, vmem),
        scratch_shapes=[
            pltpu.SemaphoreType.DMA((2, reach, 2)),
            pltpu.SemaphoreType.DMA((2, reach, 2)),
            pltpu.SemaphoreType.DMA((pairs, 2)),
            pltpu.SemaphoreType.DMA((pairs, 2)),
            pltpu.SemaphoreType.DMA((experts - 1,)),
            pltpu.SemaphoreType.DMA((experts - 1,)),
            pltpu.SemaphoreType.DMA((2,)),
        ],
        compiler_params=pltpu.CompilerParams(collective_id=0, has_side_effects=True),
    )(normed, table)


def reduce_kernel(
    experts, p_ref, o_ref, from_pair, landed, leaving, ring_send, ring_recv, pair_send, pair_recv
):
    ring = Ring(experts)
    reach = ring.pairs // 2
    rows = o_ref.shape[0] // 2
    sibling = ring.at(0, 1 - ring.core)
    meet(ring, [ring.at(1), ring.at(-1), sibling])
    toward = (1, -1)

    def cut(ref, index, h):
        return ref.at[index, pl.ds(rows * h, rows)]

    order = []
    for distance in range(reach, -1, -1):
        for h in range(2):
            for direction in (RIGHT, LEFT):
                if distance and runs(direction, h, distance, reach):
                    order.append((direction, distance, h))
    sent = []

    def go(copy):
        copy.start()
        sent.append(copy)

    def pair_copy(offset, h):
        index = offset % ring.pairs
        return remote(
            ring,
            cut(p_ref, ring.at(offset, 1 - ring.core), h),
            cut(from_pair, index, h),
            pair_send.at[index, h],
            pair_recv.at[index, h],
            sibling,
        )

    def ring_copy(direction, distance, h):
        return remote(
            ring,
            leaving.at[direction, distance - 1, pl.ds(rows * h, rows)],
            landed.at[direction, distance - 1, pl.ds(rows * h, rows)],
            ring_send.at[direction, distance - 1, h],
            ring_recv.at[direction, distance - 1, h],
            ring.at(toward[direction]),
        )

    for direction, distance, h in order:
        go(pair_copy(toward[direction] * distance, h))
    for h in range(2):
        go(pair_copy(0, h))
    for direction, distance, h in order:
        offset = toward[direction] * distance
        pair_copy(offset, h).wait_recv()
        span = pl.ds(rows * h, rows)
        total = p_ref[ring.at(offset), span].astype(jnp.float32)
        total = total + from_pair[offset % ring.pairs, span].astype(jnp.float32)
        if runs(direction, h, distance + 1, reach):
            ring_copy(direction, distance + 1, h).wait_recv()
            total = total + landed[direction, distance, span].astype(jnp.float32)
        leaving[direction, distance - 1, span] = total.astype(jnp.bfloat16)
        go(ring_copy(direction, distance, h))
    for h in range(2):
        span = pl.ds(rows * h, rows)
        pair_copy(0, h).wait_recv()
        total = p_ref[ring.me, span].astype(jnp.float32) + from_pair[0, span].astype(jnp.float32)
        for direction in (RIGHT, LEFT):
            ring_copy(direction, 1, h).wait_recv()
            total = total + landed[direction, 0, span].astype(jnp.float32)
        o_ref[span] = total.astype(o_ref.dtype)
    for copy in sent:
        copy.wait_send()


def reduce_rows(experts, pieces):
    _, rows, features = pieces.shape
    pairs, reach = experts // 2, experts // 4
    vmem = pl.BlockSpec(memory_space=pltpu.VMEM)
    return pl.pallas_call(
        functools.partial(reduce_kernel, experts),
        out_shape=jax.ShapeDtypeStruct((rows, features), pieces.dtype),
        in_specs=[vmem],
        out_specs=vmem,
        scratch_shapes=[
            pltpu.VMEM((pairs, rows, features), pieces.dtype),
            pltpu.VMEM((2, reach, rows, features), pieces.dtype),
            pltpu.VMEM((2, reach, rows, features), pieces.dtype),
            pltpu.SemaphoreType.DMA((2, reach, 2)),
            pltpu.SemaphoreType.DMA((2, reach, 2)),
            pltpu.SemaphoreType.DMA((pairs, 2)),
            pltpu.SemaphoreType.DMA((pairs, 2)),
        ],
        compiler_params=pltpu.CompilerParams(collective_id=1, has_side_effects=True),
    )(pieces)


def shards(tokens, norm_gain, w_gate, w_up, w_down, expert_ids, route_weights):
    row_count, feature_count = tokens.shape
    experts = lax.axis_size("expert")
    own_kernels = (
        lax.axis_size("tensor") == 1
        and experts % 4 == 0
        and experts >= 8
        and row_count % 32 == 0
        and row_count <= 128
    )
    stream = tokens.astype(jnp.float32)
    normed = (
        stream * lax.rsqrt(jnp.mean(stream * stream, axis=-1, keepdims=True) + epsilon) * norm_gain
    ).astype(jnp.bfloat16)
    route = route_weights / jnp.sum(route_weights, axis=-1, keepdims=True)
    numbers = jnp.arange(experts, dtype=jnp.int32)
    if own_kernels:
        chosen = expert_ids[None, :, :] == numbers[:, None, None]
        table = jnp.sum(jnp.where(chosen, route[None, :, :], 0.0), axis=2)
        table = jnp.pad(table[:, None, :], ((0, 0), (0, 7), (0, 128 - row_count)))
        rows, weights = gather_rows(experts, normed, table)
        rows = rows.reshape(experts * row_count, feature_count)
        weight = weights[:, 0, :row_count].reshape(-1, 1)
    else:
        chosen = expert_ids[:, :, None] == numbers[None, None, :]
        table = jnp.sum(jnp.where(chosen, route[:, :, None], 0.0), axis=1)
        tables = lax.all_gather(table, AXES, axis=0, tiled=True)
        rows = lax.all_gather(normed, AXES, axis=0, tiled=True)
        mine = numbers[None, :] == lax.axis_index("expert")
        weight = jnp.sum(jnp.where(mine, tables, 0.0), axis=1, keepdims=True)
    gate_pre = jnp.dot(rows, w_gate[0], preferred_element_type=jnp.float32)
    up_pre = jnp.dot(rows, w_up[0], preferred_element_type=jnp.float32)
    hidden = (jax.nn.silu(gate_pre) * up_pre).astype(jnp.bfloat16)
    out = jnp.dot(hidden, w_down[0], preferred_element_type=jnp.float32) * weight
    out = out.astype(jnp.bfloat16)
    if own_kernels:
        return reduce_rows(experts, out.reshape(experts, row_count, feature_count))
    return lax.psum_scatter(out, AXES, scatter_dimension=0, tiled=True)


def solution(mesh):
    in_specs = (
        P(("group", "expert", "tensor"), None),
        P(),
        P("expert", None, "tensor"),
        P("expert", None, "tensor"),
        P("expert", "tensor", None),
        P(("group", "expert", "tensor"), None),
        P(("group", "expert", "tensor"), None),
    )
    out_specs = P(("group", "expert", "tensor"), None)
    return jax.shard_map(shards, mesh=mesh, in_specs=in_specs, out_specs=out_specs, check_vma=False)
```

```python
import functools
import jax
import jax.numpy as jnp
from jax import lax
from jax.experimental import pallas as pl
from jax.experimental.pallas import tpu as pltpu
from jax.sharding import PartitionSpec as P

epsilon = 1e-06
AXES = ("expert", "tensor")
MESH = pl.DeviceIdType.MESH
RIGHT, LEFT = 0, 1


class Ring:
    def __init__(self, experts):
        self.pairs = experts // 2
        self.line = self.pairs // 2
        self.group = lax.axis_index("group")
        self.me = lax.axis_index("expert")
        self.core = self.me % 2
        pair = self.me // 2
        row, side = pair // 2, pair % 2
        self.pos = (1 - side) * row + side * (self.pairs - 1 - row)

    def at(self, offset, core=None):
        core = self.core if core is None else core
        place = (self.pos + offset + 2 * self.pairs) % self.pairs
        side = place // self.line
        row = (1 - side) * place + side * (self.pairs - 1 - place)
        return (row * 2 + side) * 2 + core

    def target(self, expert):
        return (self.group, expert, 0)


def remote(ring, src, dst, send_sem, recv_sem, expert):
    return pltpu.make_async_remote_copy(
        src_ref=src,
        dst_ref=dst,
        send_sem=send_sem,
        recv_sem=recv_sem,
        device_id=ring.target(expert),
        device_id_type=MESH,
    )


def runs(direction, half, distance, reach):
    return distance < reach or (distance == reach and half == direction)


def slot_of(offset, pairs):
    if offset == 0:
        return 0
    if abs(offset) * 2 == pairs:
        return pairs - 1
    return 2 * abs(offset) - (1 if offset < 0 else 0)


def block_kernel(
    experts,
    x_ref, gain_ref, picks_ref, gate_hbm, up_hbm, down_hbm, o_ref,
    gate, up, down, held, part, hidden, table, weights, from_pair, landed, leaving,
    load_sem, g_send, g_recv, gp_send, gp_recv, t_send, t_recv, r_send, r_recv, rp_send, rp_recv,
):
    ring = Ring(experts)
    pairs = ring.pairs
    reach = pairs // 2
    count, features = x_ref.shape
    ff = gate.shape[1]
    top = picks_ref.shape[0] // 2
    rows = count // 2
    sibling = ring.at(0, 1 - ring.core)
    loads = [
        pltpu.make_async_copy(source.at[0], target, load_sem.at[i])
        for i, (source, target) in enumerate(((gate_hbm, gate), (up_hbm, up), (down_hbm, down)))
    ]
    for load in loads:
        load.start()
    places = [(o, c) for o in range(-reach + 1, reach + 1) for c in range(2) if (o, c) != (0, 0)]
    barrier = pltpu.get_barrier_semaphore()
    for o, c in places:
        peer = ring.target(ring.at(o, (ring.core + c) % 2))
        pl.semaphore_signal(barrier, inc=1, device_id=peer, device_id_type=MESH)

    stream = x_ref[...].astype(jnp.float32)
    scale = lax.rsqrt(jnp.mean(stream * stream, axis=-1, keepdims=True) + epsilon)
    held[0, 0] = (stream * scale * gain_ref[...]).astype(jnp.bfloat16)
    ids = picks_ref[pl.ds(0, top)]
    route = picks_ref[pl.ds(top, top)]
    route = route / jnp.sum(route, axis=0, keepdims=True)
    for e in range(experts):
        table[e] = jnp.sum(jnp.where(ids == e, route, 0.0), axis=0, keepdims=True)
    pl.semaphore_wait(barrier, len(places))

    sent = []

    def go(copy):
        copy.start()
        sent.append(copy)

    def span(h):
        return pl.ds(rows * h, rows)

    came = (-1, 1)

    def held_at(offset, c, h):
        return held.at[slot_of(offset, pairs), c, span(h)]

    def gather_copy(direction, step, h):
        sign = came[direction]
        return remote(
            ring,
            held_at(sign * (step - 1), 0, h),
            held_at(sign * step, 0, h),
            g_send.at[direction, step - 1, h],
            g_recv.at[direction, step - 1, h],
            ring.at(-sign),
        )

    def gather_pair(offset, h):
        index = slot_of(offset, pairs)
        return remote(
            ring,
            held_at(offset, 0, h),
            held_at(offset, 1, h),
            gp_send.at[index, h],
            gp_recv.at[index, h],
            sibling,
        )

    def table_copy(index, o, c):
        expert = ring.at(o, (ring.core + c) % 2)
        back = o if abs(o) * 2 == pairs else -o
        return remote(
            ring,
            table.at[expert],
            weights.at[slot_of(back, pairs), c],
            t_send.at[slot_of(back, pairs), c],
            t_recv.at[slot_of(back, pairs), c],
            expert,
        )

    for h in range(2):
        for direction in (RIGHT, LEFT):
            go(gather_copy(direction, 1, h))
    for h in range(2):
        go(gather_pair(0, h))
    for index, (o, c) in enumerate(places):
        go(table_copy(index, o, c))

    def column(slot, c):
        line = table[ring.me] if (slot, c) == (0, 0) else weights[slot, c]
        square = jnp.broadcast_to(line, (count, count))
        same = lax.broadcasted_iota(jnp.int32, (count, count), 0) == lax.broadcasted_iota(
            jnp.int32, (count, count), 1
        )
        return jnp.sum(jnp.where(same, square, 0.0), axis=1, keepdims=True)

    def compute(first, slots):
        tall = slots * 2 * count
        hidden_tile, out_tile = 256, 512

        @pl.loop(0, ff // hidden_tile)
        def _(i):
            columns = pl.ds(pl.multiple_of(i * hidden_tile, hidden_tile), hidden_tile)
            block = held[pl.ds(first, slots)].reshape(tall, features)
            pre = jnp.dot(block, gate[:, columns], preferred_element_type=jnp.float32)
            lift = jnp.dot(block, up[:, columns], preferred_element_type=jnp.float32)
            hidden[pl.ds(0, tall), columns] = (pre / (1.0 + jnp.exp(-pre)) * lift).astype(jnp.bfloat16)

        if first == 0:
            loads[2].wait()
        for o, c in places:
            if first <= slot_of(o, pairs) < first + slots:
                index = slot_of(o, pairs)
                remote(
                    ring,
                    weights.at[index, c],
                    weights.at[index, c],
                    t_send.at[index, c],
                    t_recv.at[index, c],
                    sibling,
                ).wait_recv()
        weight = jnp.concatenate([column(first + j, c) for j in range(slots) for c in range(2)], axis=0)

        @pl.loop(0, features // out_tile)
        def _(i):
            columns = pl.ds(pl.multiple_of(i * out_tile, out_tile), out_tile)
            out = jnp.dot(hidden[pl.ds(0, tall)], down[:, columns], preferred_element_type=jnp.float32)
            out = (out * weight).astype(jnp.bfloat16).reshape(slots, 2, count, out_tile)
            part[pl.ds(first, slots), :, :, columns] = out

    toward = (1, -1)

    def reduce_pair(offset, h):
        index = slot_of(offset, pairs)
        return remote(
            ring,
            part.at[index, 1, span(h)],
            from_pair.at[index, span(h)],
            rp_send.at[index, h],
            rp_recv.at[index, h],
            sibling,
        )

    def reduce_copy(direction, distance, h):
        return remote(
            ring,
            leaving.at[direction, distance - 1, span(h)],
            landed.at[direction, distance - 1, span(h)],
            r_send.at[direction, distance - 1, h],
            r_recv.at[direction, distance - 1, h],
            ring.at(toward[direction]),
        )

    def lanes(distance):
        if distance == 0:
            return [(RIGHT, 0), (RIGHT, 1)]
        return [(d, h) for h in range(2) for d in (RIGHT, LEFT) if runs(d, h, distance, reach)]

    def settle(distance):
        for direction, h in lanes(distance):
            gather_pair(came[direction] * distance, h).wait_recv()
        if distance == 0:
            loads[0].wait()
            loads[1].wait()
        first = 0 if distance == 0 else 2 * distance - 1
        compute(first, 1 if distance in (0, reach) else 2)
        for direction, h in lanes(distance):
            go(reduce_pair(toward[direction] * distance, h))

    def pass_on(distance):
        for direction, h in lanes(distance):
            index = slot_of(toward[direction] * distance, pairs)
            reduce_pair(toward[direction] * distance, h).wait_recv()
            total = part[index, 0, span(h)].astype(jnp.float32)
            total = total + from_pair[index, span(h)].astype(jnp.float32)
            if runs(direction, h, distance + 1, reach):
                reduce_copy(direction, distance + 1, h).wait_recv()
                total = total + landed[direction, distance, span(h)].astype(jnp.float32)
            leaving[direction, distance - 1, span(h)] = total.astype(jnp.bfloat16)
            go(reduce_copy(direction, distance, h))

    for step in range(1, reach + 1):
        for direction, h in lanes(step):
            gather_copy(direction, step, h).wait_recv()
            if runs(direction, h, step + 1, reach):
                go(gather_copy(direction, step + 1, h))
            go(gather_pair(came[direction] * step, h))
        if step < reach:
            settle(step - 1)
    settle(reach)
    pass_on(reach)
    settle(reach - 1)
    for distance in range(reach - 1, 0, -1):
        pass_on(distance)
    for h in range(2):
        reduce_pair(0, h).wait_recv()
        total = part[0, 0, span(h)].astype(jnp.float32) + from_pair[0, span(h)].astype(jnp.float32)
        for direction in (RIGHT, LEFT):
            reduce_copy(direction, 1, h).wait_recv()
            total = total + landed[direction, 0, span(h)].astype(jnp.float32)
        o_ref[span(h)] = total.astype(o_ref.dtype)
    for copy in sent:
        copy.wait_send()


def expert_block(experts, tokens, gain, picks, w_gate, w_up, w_down):
    count, features = tokens.shape
    ff = w_gate.shape[2]
    pairs, reach = experts // 2, experts // 4
    bf16, f32 = jnp.bfloat16, jnp.float32
    dma = pltpu.SemaphoreType.DMA
    vmem = pl.BlockSpec(memory_space=pltpu.VMEM)
    anywhere = pl.BlockSpec(memory_space=pl.ANY)
    return pl.pallas_call(
        functools.partial(block_kernel, experts),
        out_shape=jax.ShapeDtypeStruct((count, features), bf16),
        in_specs=[vmem, vmem, vmem, anywhere, anywhere, anywhere],
        out_specs=vmem,
        scratch_shapes=[
            pltpu.VMEM((features, ff), bf16),
            pltpu.VMEM((features, ff), bf16),
            pltpu.VMEM((ff, features), bf16),
            pltpu.VMEM((pairs, 2, count, features), bf16),
            pltpu.VMEM((pairs, 2, count, features), bf16),
            pltpu.VMEM((4 * count, ff), bf16),
            pltpu.VMEM((experts, 1, count), f32),
            pltpu.VMEM((pairs, 2, 1, count), f32),
            pltpu.VMEM((pairs, count, features), bf16),
            pltpu.VMEM((2, reach, count, features), bf16),
            pltpu.VMEM((2, reach, count, features), bf16),
            dma((3,)),
            dma((2, reach, 2)),
            dma((2, reach, 2)),
            dma((pairs, 2)),
            dma((pairs, 2)),
            dma((pairs, 2)),
            dma((pairs, 2)),
            dma((2, reach, 2)),
            dma((2, reach, 2)),
            dma((pairs, 2)),
            dma((pairs, 2)),
        ],
        compiler_params=pltpu.CompilerParams(
            collective_id=0, has_side_effects=True, vmem_limit_bytes=60 * 1024 * 1024
        ),
    )(tokens, gain, picks, w_gate, w_up, w_down)


def shards(tokens, norm_gain, w_gate, w_up, w_down, expert_ids, route_weights):
    row_count, feature_count = tokens.shape
    experts = lax.axis_size("expert")
    own_kernels = (
        lax.axis_size("tensor") == 1
        and experts % 4 == 0
        and experts >= 8
        and row_count % 32 == 0
        and row_count <= 32
        and w_gate.shape[2] % 256 == 0
        and feature_count % 512 == 0
    )
    if own_kernels:
        picks = jnp.concatenate([expert_ids.astype(jnp.float32), route_weights], axis=1).T
        return expert_block(experts, tokens, norm_gain[None, :], picks, w_gate, w_up, w_down)
    stream = tokens.astype(jnp.float32)
    normed = (
        stream * lax.rsqrt(jnp.mean(stream * stream, axis=-1, keepdims=True) + epsilon) * norm_gain
    ).astype(jnp.bfloat16)
    route = route_weights / jnp.sum(route_weights, axis=-1, keepdims=True)
    numbers = jnp.arange(experts, dtype=jnp.int32)
    chosen = expert_ids[:, :, None] == numbers[None, None, :]
    table = jnp.sum(jnp.where(chosen, route[:, :, None], 0.0), axis=1)
    tables = lax.all_gather(table, AXES, axis=0, tiled=True)
    rows = lax.all_gather(normed, AXES, axis=0, tiled=True)
    mine = numbers[None, :] == lax.axis_index("expert")
    weight = jnp.sum(jnp.where(mine, tables, 0.0), axis=1, keepdims=True)
    gate_pre = jnp.dot(rows, w_gate[0], preferred_element_type=jnp.float32)
    up_pre = jnp.dot(rows, w_up[0], preferred_element_type=jnp.float32)
    hidden = (jax.nn.silu(gate_pre) * up_pre).astype(jnp.bfloat16)
    out = jnp.dot(hidden, w_down[0], preferred_element_type=jnp.float32) * weight
    out = out.astype(jnp.bfloat16)
    return lax.psum_scatter(out, AXES, scatter_dimension=0, tiled=True)


def solution(mesh):
    in_specs = (
        P(("group", "expert", "tensor"), None),
        P(),
        P("expert", None, "tensor"),
        P("expert", None, "tensor"),
        P("expert", "tensor", None),
        P(("group", "expert", "tensor"), None),
        P(("group", "expert", "tensor"), None),
    )
    out_specs = P(("group", "expert", "tensor"), None)
    return jax.shard_map(shards, mesh=mesh, in_specs=in_specs, out_specs=out_specs, check_vma=False)
```

```python
import functools
import jax
import jax.numpy as jnp
from jax import lax
from jax.experimental import pallas as pl
from jax.experimental.pallas import tpu as pltpu
from jax.sharding import PartitionSpec as P

epsilon = 1e-06
AXES = ("expert", "tensor")
MESH = pl.DeviceIdType.MESH
RIGHT, LEFT = 0, 1


class Ring:
    def __init__(self, experts):
        self.pairs = experts // 2
        self.line = self.pairs // 2
        self.group = lax.axis_index("group")
        self.me = lax.axis_index("expert")
        self.core = self.me % 2
        pair = self.me // 2
        row, side = pair // 2, pair % 2
        self.pos = (1 - side) * row + side * (self.pairs - 1 - row)

    def at(self, offset, core=None):
        core = self.core if core is None else core
        place = (self.pos + offset + 2 * self.pairs) % self.pairs
        side = place // self.line
        row = (1 - side) * place + side * (self.pairs - 1 - place)
        return (row * 2 + side) * 2 + core

    def target(self, expert):
        return (self.group, expert, 0)


def remote(ring, src, dst, send_sem, recv_sem, expert):
    return pltpu.make_async_remote_copy(
        src_ref=src,
        dst_ref=dst,
        send_sem=send_sem,
        recv_sem=recv_sem,
        device_id=ring.target(expert),
        device_id_type=MESH,
    )


def runs(direction, half, distance, reach):
    return distance < reach or (distance == reach and half == direction)


def slot_of(offset, pairs):
    if offset == 0:
        return 0
    if abs(offset) * 2 == pairs:
        return pairs - 1
    return 2 * abs(offset) - (1 if offset < 0 else 0)


def block_kernel(
    experts,
    x_ref, gain_ref, ids_ref, route_ref, gate_hbm, up_hbm, down_hbm, o_ref,
    gate, up, down, held, part, hidden, table, from_pair, landed, leaving,
    load_sem, g_send, g_recv, gp_send, gp_recv, t_send, t_recv, tp_send, tp_recv, r_send, r_recv, rp_send, rp_recv,
):
    ring = Ring(experts)
    pairs = ring.pairs
    reach = pairs // 2
    count, features = x_ref.shape
    ff = gate.shape[1]
    rows = count // 2
    sibling = ring.at(0, 1 - ring.core)
    loads = [
        pltpu.make_async_copy(source.at[0], target, load_sem.at[i])
        for i, (source, target) in enumerate(((gate_hbm, gate), (up_hbm, up), (down_hbm, down)))
    ]
    for load in loads:
        load.start()
    barrier = pltpu.get_barrier_semaphore()
    for partner in (ring.at(1), ring.at(-1), sibling):
        pl.semaphore_signal(barrier, inc=1, device_id=ring.target(partner), device_id_type=MESH)

    stream = x_ref[...].astype(jnp.float32)
    scale = lax.rsqrt(jnp.mean(stream * stream, axis=-1, keepdims=True) + epsilon)
    held[0, 0] = (stream * scale * gain_ref[...]).astype(jnp.bfloat16)
    pl.semaphore_wait(barrier, 3)

    sent = []

    def go(copy):
        copy.start()
        sent.append(copy)

    def span(h):
        return pl.ds(rows * h, rows)

    came = (-1, 1)

    def held_at(offset, c, h):
        return held.at[slot_of(offset, pairs), c, span(h)]

    def gather_copy(direction, step, h):
        sign = came[direction]
        return remote(
            ring,
            held_at(sign * (step - 1), 0, h),
            held_at(sign * step, 0, h),
            g_send.at[direction, step - 1, h],
            g_recv.at[direction, step - 1, h],
            ring.at(-sign),
        )

    def gather_pair(offset, h):
        index = slot_of(offset, pairs)
        return remote(
            ring,
            held_at(offset, 0, h),
            held_at(offset, 1, h),
            gp_send.at[index, h],
            gp_recv.at[index, h],
            sibling,
        )

    def table_copy(direction, step):
        sign = came[direction]
        return remote(
            ring,
            table.at[slot_of(sign * (step - 1), pairs), 0],
            table.at[slot_of(sign * step, pairs), 0],
            t_send.at[direction, step - 1],
            t_recv.at[direction, step - 1],
            ring.at(-sign),
        )

    def table_pair(offset):
        index = slot_of(offset, pairs)
        return remote(ring, table.at[index, 0], table.at[index, 1], tp_send.at[index], tp_recv.at[index], sibling)

    for h in range(2):
        for direction in (RIGHT, LEFT):
            go(gather_copy(direction, 1, h))
    for h in range(2):
        go(gather_pair(0, h))
    lane = lax.broadcasted_iota(jnp.int32, (count, experts), 1)
    ids = ids_ref[...]
    route = route_ref[...]
    route = route / jnp.sum(route, axis=1, keepdims=True)
    spread = jnp.zeros((count, experts), jnp.float32)
    for k in range(ids_ref.shape[1]):
        spread = spread + jnp.where(ids[:, k : k + 1] == lane, route[:, k : k + 1], 0.0)
    table[0, 0] = spread
    for direction in (RIGHT, LEFT):
        go(table_copy(direction, 1))
    go(table_pair(0))

    def column(slot, c):
        return jnp.sum(jnp.where(lane == ring.me, table[slot, c], 0.0), axis=1, keepdims=True)

    def compute(first, slots, between):
        tall = slots * 2 * count
        hidden_tile, out_tile = 256, 512

        @pl.loop(0, ff // hidden_tile)
        def _(i):
            columns = pl.ds(pl.multiple_of(i * hidden_tile, hidden_tile), hidden_tile)
            block = held[pl.ds(first, slots)].reshape(tall, features)
            pre = jnp.dot(block, gate[:, columns], preferred_element_type=jnp.float32)
            lift = jnp.dot(block, up[:, columns], preferred_element_type=jnp.float32)
            hidden[pl.ds(0, tall), columns] = (pre / (1.0 + jnp.exp(-pre)) * lift).astype(jnp.bfloat16)

        between()
        if first == 0:
            loads[2].wait()
        weight = jnp.concatenate([column(first + j, c) for j in range(slots) for c in range(2)], axis=0)

        @pl.loop(0, features // out_tile)
        def _(i):
            columns = pl.ds(pl.multiple_of(i * out_tile, out_tile), out_tile)
            out = jnp.dot(hidden[pl.ds(0, tall)], down[:, columns], preferred_element_type=jnp.float32)
            out = (out * weight).astype(jnp.bfloat16).reshape(slots, 2, count, out_tile)
            part[pl.ds(first, slots), :, :, columns] = out

    toward = (1, -1)

    def reduce_pair(offset, h):
        index = slot_of(offset, pairs)
        return remote(
            ring,
            part.at[index, 1, span(h)],
            from_pair.at[index, span(h)],
            rp_send.at[index, h],
            rp_recv.at[index, h],
            sibling,
        )

    def reduce_copy(direction, distance, h):
        return remote(
            ring,
            leaving.at[direction, distance - 1, span(h)],
            landed.at[direction, distance - 1, span(h)],
            r_send.at[direction, distance - 1, h],
            r_recv.at[direction, distance - 1, h],
            ring.at(toward[direction]),
        )

    def lanes(distance):
        if distance == 0:
            return [(RIGHT, 0), (RIGHT, 1)]
        return [(d, h) for h in range(2) for d in (RIGHT, LEFT) if runs(d, h, distance, reach)]

    def offsets(distance):
        return (distance,) if distance in (0, reach) else (-distance, distance)

    def settle(distance, between=lambda: None):
        for direction, h in lanes(distance):
            gather_pair(came[direction] * distance, h).wait_recv()
        for offset in offsets(distance):
            table_pair(offset).wait_recv()
        if distance == 0:
            loads[0].wait()
            loads[1].wait()
        first = 0 if distance == 0 else 2 * distance - 1
        compute(first, 1 if distance in (0, reach) else 2, between)
        for direction, h in lanes(distance):
            go(reduce_pair(toward[direction] * distance, h))

    def pass_on(distance):
        for direction, h in lanes(distance):
            index = slot_of(toward[direction] * distance, pairs)
            reduce_pair(toward[direction] * distance, h).wait_recv()
            total = part[index, 0, span(h)].astype(jnp.float32)
            total = total + from_pair[index, span(h)].astype(jnp.float32)
            if runs(direction, h, distance + 1, reach):
                reduce_copy(direction, distance + 1, h).wait_recv()
                total = total + landed[direction, distance, span(h)].astype(jnp.float32)
            leaving[direction, distance - 1, span(h)] = total.astype(jnp.bfloat16)
            go(reduce_copy(direction, distance, h))

    def forward(step, half):
        for direction, h in lanes(step):
            if h != half:
                continue
            gather_copy(direction, step, h).wait_recv()
            if runs(direction, h, step + 1, reach):
                go(gather_copy(direction, step + 1, h))
            go(gather_pair(came[direction] * step, h))
            if h == 0 and not (step == reach and direction == LEFT):
                table_copy(direction, step).wait_recv()
                if step + 1 < reach or (step + 1 == reach and direction == RIGHT):
                    go(table_copy(direction, step + 1))
                go(table_pair(came[direction] * step))

    forward(1, 0)
    forward(1, 1)
    settle(0)
    for step in range(2, reach):
        forward(step, 0)
        settle(step - 1, functools.partial(forward, step, 1))
    forward(reach, 0)
    forward(reach, 1)
    settle(reach)
    pass_on(reach)
    settle(reach - 1)
    for distance in range(reach - 1, 0, -1):
        pass_on(distance)
    for h in range(2):
        reduce_pair(0, h).wait_recv()
        total = part[0, 0, span(h)].astype(jnp.float32) + from_pair[0, span(h)].astype(jnp.float32)
        for direction in (RIGHT, LEFT):
            reduce_copy(direction, 1, h).wait_recv()
            total = total + landed[direction, 0, span(h)].astype(jnp.float32)
        o_ref[span(h)] = total.astype(o_ref.dtype)
    for copy in sent:
        copy.wait_send()


def expert_block(experts, tokens, gain, ids, route, w_gate, w_up, w_down):
    count, features = tokens.shape
    ff = w_gate.shape[2]
    pairs, reach = experts // 2, experts // 4
    bf16, f32 = jnp.bfloat16, jnp.float32
    dma = pltpu.SemaphoreType.DMA
    vmem = pl.BlockSpec(memory_space=pltpu.VMEM)
    anywhere = pl.BlockSpec(memory_space=pl.ANY)
    return pl.pallas_call(
        functools.partial(block_kernel, experts),
        out_shape=jax.ShapeDtypeStruct((count, features), bf16),
        in_specs=[vmem, vmem, vmem, vmem, anywhere, anywhere, anywhere],
        out_specs=vmem,
        scratch_shapes=[
            pltpu.VMEM((features, ff), bf16),
            pltpu.VMEM((features, ff), bf16),
            pltpu.VMEM((ff, features), bf16),
            pltpu.VMEM((pairs, 2, count, features), bf16),
            pltpu.VMEM((pairs, 2, count, features), bf16),
            pltpu.VMEM((4 * count, ff), bf16),
            pltpu.VMEM((pairs, 2, count, experts), f32),
            pltpu.VMEM((pairs, count, features), bf16),
            pltpu.VMEM((2, reach, count, features), bf16),
            pltpu.VMEM((2, reach, count, features), bf16),
            dma((3,)),
            dma((2, reach, 2)),
            dma((2, reach, 2)),
            dma((pairs, 2)),
            dma((pairs, 2)),
            dma((2, reach)),
            dma((2, reach)),
            dma((pairs,)),
            dma((pairs,)),
            dma((2, reach, 2)),
            dma((2, reach, 2)),
            dma((pairs, 2)),
            dma((pairs, 2)),
        ],
        compiler_params=pltpu.CompilerParams(
            collective_id=0, has_side_effects=True, vmem_limit_bytes=60 * 1024 * 1024
        ),
    )(tokens, gain, ids, route, w_gate, w_up, w_down)


def shards(tokens, norm_gain, w_gate, w_up, w_down, expert_ids, route_weights):
    row_count, feature_count = tokens.shape
    experts = lax.axis_size("expert")
    own_kernels = (
        lax.axis_size("tensor") == 1
        and experts % 4 == 0
        and experts >= 8
        and row_count % 32 == 0
        and row_count <= 32
        and w_gate.shape[2] % 256 == 0
        and feature_count % 512 == 0
    )
    if own_kernels:
        return expert_block(experts, tokens, norm_gain[None, :], expert_ids, route_weights, w_gate, w_up, w_down)
    stream = tokens.astype(jnp.float32)
    normed = (
        stream * lax.rsqrt(jnp.mean(stream * stream, axis=-1, keepdims=True) + epsilon) * norm_gain
    ).astype(jnp.bfloat16)
    route = route_weights / jnp.sum(route_weights, axis=-1, keepdims=True)
    numbers = jnp.arange(experts, dtype=jnp.int32)
    chosen = expert_ids[:, :, None] == numbers[None, None, :]
    table = jnp.sum(jnp.where(chosen, route[:, :, None], 0.0), axis=1)
    tables = lax.all_gather(table, AXES, axis=0, tiled=True)
    rows = lax.all_gather(normed, AXES, axis=0, tiled=True)
    mine = numbers[None, :] == lax.axis_index("expert")
    weight = jnp.sum(jnp.where(mine, tables, 0.0), axis=1, keepdims=True)
    gate_pre = jnp.dot(rows, w_gate[0], preferred_element_type=jnp.float32)
    up_pre = jnp.dot(rows, w_up[0], preferred_element_type=jnp.float32)
    hidden = (jax.nn.silu(gate_pre) * up_pre).astype(jnp.bfloat16)
    out = jnp.dot(hidden, w_down[0], preferred_element_type=jnp.float32) * weight
    out = out.astype(jnp.bfloat16)
    return lax.psum_scatter(out, AXES, scatter_dimension=0, tiled=True)


def solution(mesh):
    in_specs = (
        P(("group", "expert", "tensor"), None),
        P(),
        P("expert", None, "tensor"),
        P("expert", None, "tensor"),
        P("expert", "tensor", None),
        P(("group", "expert", "tensor"), None),
        P(("group", "expert", "tensor"), None),
    )
    out_specs = P(("group", "expert", "tensor"), None)
    return jax.shard_map(shards, mesh=mesh, in_specs=in_specs, out_specs=out_specs, check_vma=False)
```

```python
import functools
import jax
import jax.numpy as jnp
from jax import lax
from jax.experimental import pallas as pl
from jax.experimental.pallas import tpu as pltpu
from jax.sharding import PartitionSpec as P

epsilon = 1e-06
AXES = ("expert", "tensor")
MESH = pl.DeviceIdType.MESH
RIGHT, LEFT = 0, 1


class Ring:
    def __init__(self, experts):
        self.pairs = experts // 2
        self.line = self.pairs // 2
        self.group = lax.axis_index("group")
        self.me = lax.axis_index("expert")
        self.core = self.me % 2
        pair = self.me // 2
        row, side = pair // 2, pair % 2
        self.pos = (1 - side) * row + side * (self.pairs - 1 - row)

    def at(self, offset, core=None):
        core = self.core if core is None else core
        place = (self.pos + offset + 2 * self.pairs) % self.pairs
        side = place // self.line
        row = (1 - side) * place + side * (self.pairs - 1 - place)
        return (row * 2 + side) * 2 + core

    def target(self, expert):
        return (self.group, expert, 0)


def remote(ring, src, dst, send_sem, recv_sem, expert):
    return pltpu.make_async_remote_copy(
        src_ref=src,
        dst_ref=dst,
        send_sem=send_sem,
        recv_sem=recv_sem,
        device_id=ring.target(expert),
        device_id_type=MESH,
    )


def runs(direction, half, distance, reach):
    return distance < reach or (distance == reach and half == direction)


def slot_of(offset, pairs):
    if offset == 0:
        return 0
    if abs(offset) * 2 == pairs:
        return pairs - 1
    return 2 * abs(offset) - (1 if offset < 0 else 0)


def block_kernel(
    experts,
    x_ref, gain_ref, ids_ref, route_ref, gate_hbm, up_hbm, down_hbm, o_ref,
    gate, up, down, held, part, hidden, table, from_pair, landed, leaving,
    load_sem, g_send, g_recv, gp_send, gp_recv, t_send, t_recv, tp_send, tp_recv, r_send, r_recv, rp_send, rp_recv,
):
    ring = Ring(experts)
    pairs = ring.pairs
    reach = pairs // 2
    count, features = x_ref.shape
    ff = gate.shape[1]
    rows = count // 2
    sibling = ring.at(0, 1 - ring.core)
    loads = [
        pltpu.make_async_copy(source.at[0], target, load_sem.at[i])
        for i, (source, target) in enumerate(((gate_hbm, gate), (up_hbm, up), (down_hbm, down)))
    ]
    for load in loads:
        load.start()
    barrier = pltpu.get_barrier_semaphore()
    for partner in (ring.at(1), ring.at(-1), sibling):
        pl.semaphore_signal(barrier, inc=1, device_id=ring.target(partner), device_id_type=MESH)

    stream = x_ref[...].astype(jnp.float32)
    scale = lax.rsqrt(jnp.mean(stream * stream, axis=-1, keepdims=True) + epsilon)
    held[0, 0] = (stream * scale * gain_ref[...]).astype(jnp.bfloat16)
    pl.semaphore_wait(barrier, 3)

    sent = []

    def go(copy):
        copy.start()
        sent.append(copy)

    def span(h):
        return pl.ds(rows * h, rows)

    came = (-1, 1)

    def held_at(offset, c, h):
        return held.at[slot_of(offset, pairs), c, span(h)]

    def gather_copy(direction, step, h):
        sign = came[direction]
        return remote(
            ring,
            held_at(sign * (step - 1), 0, h),
            held_at(sign * step, 0, h),
            g_send.at[direction, step - 1, h],
            g_recv.at[direction, step - 1, h],
            ring.at(-sign),
        )

    def gather_pair(offset, h):
        index = slot_of(offset, pairs)
        return remote(
            ring,
            held_at(offset, 0, h),
            held_at(offset, 1, h),
            gp_send.at[index, h],
            gp_recv.at[index, h],
            sibling,
        )

    def table_copy(direction, step):
        sign = came[direction]
        return remote(
            ring,
            table.at[slot_of(sign * (step - 1), pairs), 0],
            table.at[slot_of(sign * step, pairs), 0],
            t_send.at[direction, step - 1],
            t_recv.at[direction, step - 1],
            ring.at(-sign),
        )

    def table_pair(offset):
        index = slot_of(offset, pairs)
        return remote(ring, table.at[index, 0], table.at[index, 1], tp_send.at[index], tp_recv.at[index], sibling)

    for h in range(2):
        for direction in (RIGHT, LEFT):
            go(gather_copy(direction, 1, h))
    for h in range(2):
        go(gather_pair(0, h))
    lane = lax.broadcasted_iota(jnp.int32, (count, experts), 1)
    square = (count, count)
    same = lax.broadcasted_iota(jnp.int32, square, 0) == lax.broadcasted_iota(jnp.int32, square, 1)

    def upright(line):
        return jnp.sum(jnp.where(same, jnp.broadcast_to(line, square), 0.0), axis=1, keepdims=True)

    ids = ids_ref[...].astype(jnp.float32)
    route = route_ref[...]
    route = route / jnp.sum(route, axis=0, keepdims=True)
    spread = jnp.zeros((count, experts), jnp.float32)
    for k in range(ids_ref.shape[0]):
        hit = upright(ids[k : k + 1]) == lane.astype(jnp.float32)
        spread = spread + jnp.where(hit, upright(route[k : k + 1]), 0.0)
    table[0, 0] = spread
    for direction in (RIGHT, LEFT):
        go(table_copy(direction, 1))
    go(table_pair(0))

    def column(slot, c):
        return jnp.sum(jnp.where(lane == ring.me, table[slot, c], 0.0), axis=1, keepdims=True)

    def compute(first, slots, between):
        tall = slots * 2 * count
        hidden_tile, out_tile = 256, 512

        @pl.loop(0, ff // hidden_tile)
        def _(i):
            columns = pl.ds(pl.multiple_of(i * hidden_tile, hidden_tile), hidden_tile)
            block = held[pl.ds(first, slots)].reshape(tall, features)
            pre = jnp.dot(block, gate[:, columns], preferred_element_type=jnp.float32)
            lift = jnp.dot(block, up[:, columns], preferred_element_type=jnp.float32)
            hidden[pl.ds(0, tall), columns] = (pre / (1.0 + jnp.exp(-pre)) * lift).astype(jnp.bfloat16)

        between()
        if first == 0:
            loads[2].wait()
        weight = jnp.concatenate([column(first + j, c) for j in range(slots) for c in range(2)], axis=0)

        @pl.loop(0, features // out_tile)
        def _(i):
            columns = pl.ds(pl.multiple_of(i * out_tile, out_tile), out_tile)
            out = jnp.dot(hidden[pl.ds(0, tall)], down[:, columns], preferred_element_type=jnp.float32)
            out = (out * weight).astype(jnp.bfloat16).reshape(slots, 2, count, out_tile)
            part[pl.ds(first, slots), :, :, columns] = out

    toward = (1, -1)

    def reduce_pair(offset, h):
        index = slot_of(offset, pairs)
        return remote(
            ring,
            part.at[index, 1, span(h)],
            from_pair.at[index, span(h)],
            rp_send.at[index, h],
            rp_recv.at[index, h],
            sibling,
        )

    def reduce_copy(direction, distance, h):
        return remote(
            ring,
            leaving.at[direction, distance - 1, span(h)],
            landed.at[direction, distance - 1, span(h)],
            r_send.at[direction, distance - 1, h],
            r_recv.at[direction, distance - 1, h],
            ring.at(toward[direction]),
        )

    def lanes(distance):
        if distance == 0:
            return [(RIGHT, 0), (RIGHT, 1)]
        return [(d, h) for h in range(2) for d in (RIGHT, LEFT) if runs(d, h, distance, reach)]

    def offsets(distance):
        return (distance,) if distance in (0, reach) else (-distance, distance)

    def settle(distance, between=lambda: None):
        for direction, h in lanes(distance):
            gather_pair(came[direction] * distance, h).wait_recv()
        for offset in offsets(distance):
            table_pair(offset).wait_recv()
        if distance == 0:
            loads[0].wait()
            loads[1].wait()
        first = 0 if distance == 0 else 2 * distance - 1
        compute(first, 1 if distance in (0, reach) else 2, between)
        for direction, h in lanes(distance):
            go(reduce_pair(toward[direction] * distance, h))

    def pass_on(distance):
        for direction, h in lanes(distance):
            index = slot_of(toward[direction] * distance, pairs)
            reduce_pair(toward[direction] * distance, h).wait_recv()
            total = part[index, 0, span(h)].astype(jnp.float32)
            total = total + from_pair[index, span(h)].astype(jnp.float32)
            if runs(direction, h, distance + 1, reach):
                reduce_copy(direction, distance + 1, h).wait_recv()
                total = total + landed[direction, distance, span(h)].astype(jnp.float32)
            leaving[direction, distance - 1, span(h)] = total.astype(jnp.bfloat16)
            go(reduce_copy(direction, distance, h))

    def forward(step, half):
        for direction, h in lanes(step):
            if h != half:
                continue
            gather_copy(direction, step, h).wait_recv()
            if runs(direction, h, step + 1, reach):
                go(gather_copy(direction, step + 1, h))
            go(gather_pair(came[direction] * step, h))
            if h == 0 and not (step == reach and direction == LEFT):
                table_copy(direction, step).wait_recv()
                if step + 1 < reach or (step + 1 == reach and direction == RIGHT):
                    go(table_copy(direction, step + 1))
                go(table_pair(came[direction] * step))

    forward(1, 0)
    forward(1, 1)
    settle(0)
    for step in range(2, reach):
        forward(step, 0)
        settle(step - 1, functools.partial(forward, step, 1))
    forward(reach, 0)
    forward(reach, 1)
    settle(reach)
    pass_on(reach)
    settle(reach - 1)
    for distance in range(reach - 1, 0, -1):
        pass_on(distance)
    for h in range(2):
        reduce_pair(0, h).wait_recv()
        total = part[0, 0, span(h)].astype(jnp.float32) + from_pair[0, span(h)].astype(jnp.float32)
        for direction in (RIGHT, LEFT):
            reduce_copy(direction, 1, h).wait_recv()
            total = total + landed[direction, 0, span(h)].astype(jnp.float32)
        o_ref[span(h)] = total.astype(o_ref.dtype)
    for copy in sent:
        copy.wait_send()


def expert_block(experts, tokens, gain, ids, route, w_gate, w_up, w_down):
    count, features = tokens.shape
    ff = w_gate.shape[2]
    pairs, reach = experts // 2, experts // 4
    bf16, f32 = jnp.bfloat16, jnp.float32
    dma = pltpu.SemaphoreType.DMA
    vmem = pl.BlockSpec(memory_space=pltpu.VMEM)
    anywhere = pl.BlockSpec(memory_space=pl.ANY)
    return pl.pallas_call(
        functools.partial(block_kernel, experts),
        out_shape=jax.ShapeDtypeStruct((count, features), bf16),
        in_specs=[vmem, vmem, vmem, vmem, anywhere, anywhere, anywhere],
        out_specs=vmem,
        scratch_shapes=[
            pltpu.VMEM((features, ff), bf16),
            pltpu.VMEM((features, ff), bf16),
            pltpu.VMEM((ff, features), bf16),
            pltpu.VMEM((pairs, 2, count, features), bf16),
            pltpu.VMEM((pairs, 2, count, features), bf16),
            pltpu.VMEM((4 * count, ff), bf16),
            pltpu.VMEM((pairs, 2, count, experts), f32),
            pltpu.VMEM((pairs, count, features), bf16),
            pltpu.VMEM((2, reach, count, features), bf16),
            pltpu.VMEM((2, reach, count, features), bf16),
            dma((3,)),
            dma((2, reach, 2)),
            dma((2, reach, 2)),
            dma((pairs, 2)),
            dma((pairs, 2)),
            dma((2, reach)),
            dma((2, reach)),
            dma((pairs,)),
            dma((pairs,)),
            dma((2, reach, 2)),
            dma((2, reach, 2)),
            dma((pairs, 2)),
            dma((pairs, 2)),
        ],
        compiler_params=pltpu.CompilerParams(
            collective_id=0, has_side_effects=True, vmem_limit_bytes=60 * 1024 * 1024
        ),
    )(tokens, gain, ids, route, w_gate, w_up, w_down)


def shards(tokens, norm_gain, w_gate, w_up, w_down, expert_ids, route_weights):
    row_count, feature_count = tokens.shape
    experts = lax.axis_size("expert")
    own_kernels = (
        lax.axis_size("tensor") == 1
        and experts % 4 == 0
        and experts >= 8
        and row_count % 32 == 0
        and row_count <= 32
        and w_gate.shape[2] % 256 == 0
        and feature_count % 512 == 0
    )
    if own_kernels:
        ids, route = expert_ids.T, route_weights.T
        return expert_block(experts, tokens, norm_gain[None, :], ids, route, w_gate, w_up, w_down)
    stream = tokens.astype(jnp.float32)
    normed = (
        stream * lax.rsqrt(jnp.mean(stream * stream, axis=-1, keepdims=True) + epsilon) * norm_gain
    ).astype(jnp.bfloat16)
    route = route_weights / jnp.sum(route_weights, axis=-1, keepdims=True)
    numbers = jnp.arange(experts, dtype=jnp.int32)
    chosen = expert_ids[:, :, None] == numbers[None, None, :]
    table = jnp.sum(jnp.where(chosen, route[:, :, None], 0.0), axis=1)
    tables = lax.all_gather(table, AXES, axis=0, tiled=True)
    rows = lax.all_gather(normed, AXES, axis=0, tiled=True)
    mine = numbers[None, :] == lax.axis_index("expert")
    weight = jnp.sum(jnp.where(mine, tables, 0.0), axis=1, keepdims=True)
    gate_pre = jnp.dot(rows, w_gate[0], preferred_element_type=jnp.float32)
    up_pre = jnp.dot(rows, w_up[0], preferred_element_type=jnp.float32)
    hidden = (jax.nn.silu(gate_pre) * up_pre).astype(jnp.bfloat16)
    out = jnp.dot(hidden, w_down[0], preferred_element_type=jnp.float32) * weight
    out = out.astype(jnp.bfloat16)
    return lax.psum_scatter(out, AXES, scatter_dimension=0, tiled=True)


def solution(mesh):
    in_specs = (
        P(("group", "expert", "tensor"), None),
        P(),
        P("expert", None, "tensor"),
        P("expert", None, "tensor"),
        P("expert", "tensor", None),
        P(("group", "expert", "tensor"), None),
        P(("group", "expert", "tensor"), None),
    )
    out_specs = P(("group", "expert", "tensor"), None)
    return jax.shard_map(shards, mesh=mesh, in_specs=in_specs, out_specs=out_specs, check_vma=False)
```
